32 devices in a mesh: hist: 8 (over z, x), cand: 4 (over y, core).
Axes of the slice: x: 2, y: 2, z: 4, core: 2. Of those that a mesh axis runs over, the one named last changes fastest.
Arguments:
- cand_emb: bfloat16 [4, 256, 1024], P('cand', 'hist'), may hold values from -6 to 6
- cand_user: int32 [4, 256], P('cand'), may hold values from 0 to 3
- kv_cache: bfloat16 [4, 64, 2, 128, 1024], P('cand', 'hist'), may hold values from -6 to 6
- tile_user: int32 [4, 64], P('cand', 'hist'), may hold values from 0 to 3
- tile_len: int32 [4, 64], P('cand', 'hist'), may hold values from 1 to 128
- w_uq: bfloat16 [2048, 1024], P('cand'), may hold values from -0.1875 to 0.1875
- w_out: bfloat16 [1024, 1024], P('cand'), may hold values from -0.1875 to 0.1875
Outputs:
- scored: bfloat16 [4, 256, 1024], P('cand', 'hist')
The draws below stay inside these ranges and needn't reach their ends.
All inputs are finite; a program needn't handle non-finite values.
Results may differ from the reference program's by a relative error of at most 0.0053.
Values may be sent and summed in bfloat16 or wider, within the bound.
A program may use at most 128 MiB of HBM per device.

```python
import math
import jax
import jax.numpy as jnp
import numpy as np
from jax import lax

D = 1024
HEADS = 8
TILE_ROWS = 128
TILE_DEV = 8
USERS_GRP = 4
GROUPS = 4
CANDS_GRP = 256
TILES_GRP = 64


def place_ends(values, stream_key, low, largest):
    longest = values.shape.index(max(values.shape))
    spots = []
    for shift in (0, 1):
        where = [jax.random.randint(jax.random.fold_in(stream_key, axis), (), 0, length) for axis, length in enumerate(values.shape)]
        where[longest] = (where[longest] + shift) % values.shape[longest]
        spots.append(tuple(where))
    return values.at[spots[0]].set(low).at[spots[1]].set(largest)


def block_levels(rng, shape, split, least, top_value):
    loudness = 1.0
    for position, blocks in split:
        heights = jax.random.uniform(jax.random.fold_in(jax.random.fold_in(rng, 6), position), (blocks,), jnp.float32, least / len(split), top_value / len(split))
        loudness = loudness * jnp.repeat(jnp.exp(heights), shape[position] // blocks).reshape((-1,) + (1,) * (len(shape) - 1 - position))
    return loudness


def rank_table(number_of, slope):
    portions = [(1 << 20) // math.isqrt(rank ** slope) + 1 for rank in range(1, number_of + 1)]
    scale = 1 + sum(portions) // (1 << 30)
    return np.cumsum(np.array([max(1, weight // scale) for weight in portions]))


def skewed_ids(own_key, shape, amount, lean):
    grid = rank_table(amount, lean)
    lot = jax.random.randint(jax.random.fold_in(own_key, 1), shape, 0, int(grid[amount - 1]))
    grade = jnp.searchsorted(jnp.asarray(grid, jnp.int32), lot, side="right")
    return jax.random.permutation(jax.random.fold_in(own_key, 2), amount)[grade].astype(jnp.int32)


def centred(key, dims, scale, bound, shards=(), held_as=jnp.bfloat16):
    array = scale * jax.random.normal(key, dims, jnp.float32)
    if shards:
        array = array * block_levels(key, dims, shards, -0.22, 0.18)
    return jnp.clip(array, -bound, bound).astype(held_as)


def setup_inputs(seed: int = 0) -> dict:
    seeds = jax.random.split(jax.random.key(seed), 8)
    return {
        "cand_emb": centred(seeds[0], (GROUPS, CANDS_GRP, D), 1.0, 6.0, ((0, 4), (1, 8))),
        "cand_user": place_ends(skewed_ids(seeds[1], (GROUPS, CANDS_GRP), USERS_GRP, 2), jax.random.fold_in(seeds[1], 3), 0, USERS_GRP - 1).astype(jnp.int32),
        "kv_cache": centred(seeds[2], (GROUPS, TILES_GRP, 2, TILE_ROWS, D), 1.0, 6.0, ((0, 4), (1, 8))),
        "tile_user": place_ends(jax.random.randint(seeds[3], (GROUPS, TILES_GRP), 0, USERS_GRP), jax.random.fold_in(seeds[3], 1), 0, USERS_GRP - 1).astype(jnp.int32),
        "tile_len": place_ends(jax.random.randint(seeds[4], (GROUPS, TILES_GRP), 1, TILE_ROWS + 1), jax.random.fold_in(seeds[4], 1), 1, TILE_ROWS).astype(jnp.int32),
        "w_uq": centred(seeds[5], (2 * D, D), D ** -0.5, 0.1875, ((0, 4),)),
        "w_out": centred(seeds[6], (D, D), D ** -0.5, 0.1875, ((0, 4),)),
    }


def reference(cand_emb, cand_user, kv_cache, tile_user, tile_len, w_uq, w_out):
    head_size = D // HEADS
    score_scale = 1.0 / head_size ** 0.5

    def one_group(inputs):
        embeds, users, caches, owners, lengths = inputs
        count = embeds.shape[0]
        uq_full = jnp.dot(embeds, w_uq.T, preferred_element_type=jnp.float32)
        uq_full = jax.nn.silu(uq_full).astype(jnp.bfloat16)
        u_part = uq_full[:, :D]
        queries = uq_full[:, D:].astype(jnp.float32).reshape(count, HEADS, head_size)
        blocks = caches.reshape(TILES_GRP // TILE_DEV, TILE_DEV, 2, TILE_ROWS, D)
        block_owner = owners.reshape(TILES_GRP // TILE_DEV, TILE_DEV)
        block_len = lengths.reshape(TILES_GRP // TILE_DEV, TILE_DEV)
        row_ids = jnp.arange(TILE_ROWS, dtype=jnp.int32)

        def step(total, item):
            block, who, lens = item
            keys = block[:, 0].astype(jnp.float32).reshape(TILE_DEV * TILE_ROWS, HEADS, head_size)
            values = block[:, 1].astype(jnp.float32).reshape(TILE_DEV * TILE_ROWS, HEADS, head_size)
            valid = (row_ids[None, :] < lens[:, None]).reshape(TILE_DEV * TILE_ROWS)
            whose = jnp.repeat(who, TILE_ROWS)
            allowed = (users[:, None] == whose[None, :]) & valid[None, :]
            scores = jnp.einsum('qhd,khd->hqk', queries, keys) * score_scale
            weights = jnp.where(allowed[None], jax.nn.silu(scores), 0.0).astype(jnp.bfloat16)
            weights = lax.optimization_barrier(weights).astype(jnp.float32)
            return (total + jnp.einsum('hqk,khd->qhd', weights, values), None)
        start_total = jnp.zeros((count, HEADS, head_size), jnp.float32)
        attn, _ = lax.scan(step, start_total, (blocks, block_owner, block_len))
        attn = attn.reshape(count, D)
        center = lax.optimization_barrier(jnp.mean(attn, axis=1, keepdims=True))
        spread = lax.optimization_barrier(jnp.mean((attn - center) ** 2, axis=1, keepdims=True))
        normed = (attn - center) / jnp.sqrt(spread + 1e-05)
        y_rows = (normed * u_part.astype(jnp.float32)).astype(jnp.bfloat16)
        projected = jnp.dot(y_rows, w_out.T, preferred_element_type=jnp.float32)
        return (embeds.astype(jnp.float32) + projected).astype(jnp.bfloat16)
    return lax.map(one_group, (cand_emb, cand_user, kv_cache, tile_user, tile_len))
```

```python
import functools

import jax
import jax.numpy as jnp
from jax import lax
from jax.experimental import pallas as pl
from jax.experimental.pallas import tpu as pltpu
from jax.sharding import PartitionSpec as P

HEADS = 8
PIECES = 2
DIRECT = 1
BF16 = jnp.bfloat16
F32 = jnp.float32


def times_rows(left, slab):
    return lax.dot_general(left, slab, (((1,), (1,)), ((), ())), preferred_element_type=F32)


def half_silu(half):
    return half + half * jnp.tanh(half)


def flip(index, bits):
    bit = 1
    while bit <= bits:
        if bits & bit:
            index = index + bit * (1 - 2 * lax.rem(index // bit, 2))
        bit *= 2
    return index


def kernel(
    nx, nz, nc, emb_hbm, user_hbm, kv_hbm, owner_hbm, len_hbm, wuq_hbm, wout_hbm, out_ref,
    user_ref, owner_ref, len_ref, embs, kv, wuq, wout, q_ret, q_all, u_own, u_send, mask, part, landed,
    local_sem, emb_sem, wuq_ssem, wuq_rsem, ret_ssem, ret_rsem, far_ssem, z_ssem, z_rsem, x_ssem, x_rsem,
    part_ssem, part_rsem, u_sem, w_ssem, w_rsem, wp_ssem, wp_rsem, wf_ssem, wf_rsem, news,
):
    nh = nx * nz
    hist = lax.axis_index("hist")
    z, x = hist // nx, lax.rem(hist, nx)
    cand = lax.axis_index("cand")
    side = nc // 2
    is_q = cand >= side
    partner = lax.rem(cand + side, nc)
    place = lax.rem(cand, side)
    base = cand - place
    rows, width = embs.shape[1], embs.shape[2]
    head_size = width // HEADS
    tiles, tile_rows = kv.shape[0], kv.shape[2]
    keys = tiles * tile_rows
    span = width // PIECES
    half = nz // 2

    def remote(src, dst, ssem, rsem, peer):
        return pltpu.make_async_remote_copy(
            src_ref=src, dst_ref=dst, send_sem=ssem, recv_sem=rsem,
            device_id=peer, device_id_type=pl.DeviceIdType.MESH,
        )

    def at(s, t):
        return flip(z, s) * nx + flip(x, t)

    def mate(step):
        return base + lax.rem(place + step, side)

    def signal(sem, hist_to, cand_to):
        pl.semaphore_signal(
            sem, inc=1, device_id=(hist_to, cand_to), device_id_type=pl.DeviceIdType.MESH
        )

    load_emb = pltpu.make_async_copy(emb_hbm.at[0], embs.at[0], local_sem.at[0])
    load_wuq = pltpu.make_async_copy(wuq_hbm, wuq.at[place], local_sem.at[1])
    load_kv = pltpu.make_async_copy(kv_hbm.at[0], kv, local_sem.at[2])
    load_wout = pltpu.make_async_copy(wout_hbm, wout.at[cand], local_sem.at[3])
    load_small = [
        pltpu.make_async_copy(src, dst, local_sem.at[4 + index])
        for index, (src, dst) in enumerate(
            ((user_hbm, user_ref), (owner_hbm, owner_ref), (len_hbm, len_ref))
        )
    ]
    barrier = pltpu.get_barrier_semaphore()
    low, high = z > 0, z < nz - 1
    signal(barrier, hist, partner)
    for step in range(1, side):
        signal(barrier, hist, mate(step))
    for t in range(1, nx):
        signal(barrier, at(0, t), cand)
    pl.when(low)(lambda: signal(barrier, hist - nx, cand))
    pl.when(high)(lambda: signal(barrier, hist + nx, cand))
    load_emb.start()
    load_wuq.start()
    for load in load_small:
        load.start()
    load_wout.start()
    load_kv.start()
    pl.semaphore_wait(
        barrier, 1 + side - 1 + nx - 1 + low.astype(jnp.int32) + high.astype(jnp.int32)
    )

    emb_copy = remote(emb_hbm.at[0], embs.at[1], emb_sem.at[0], emb_sem.at[1], (hist, partner))
    emb_copy.start()

    def wuq_copy(step):
        return remote(
            wuq_hbm, wuq.at[place], wuq_ssem.at[step], wuq_rsem.at[step], (hist, mate(step))
        )

    for step in range(1, side):
        wuq_copy(step).start()

    outs = wout.shape[1]
    cuts = (0, outs // 4, outs)

    def w_copy(step):
        return remote(wout_hbm, wout.at[cand], w_ssem.at[step], w_rsem.at[step], (hist, mate(step)))

    def wp_copy(chunk):
        lines = pl.ds(cuts[chunk], cuts[chunk + 1] - cuts[chunk])
        return remote(
            wout_hbm.at[lines], wout.at[cand, lines], wp_ssem.at[chunk], wp_rsem.at[chunk],
            (hist, partner),
        )

    def wf_copy(step):
        return remote(
            wout.at[partner], wout.at[partner], wf_ssem.at[step], wf_rsem.at[step],
            (hist, mate(step)),
        )

    wp_copy(0).start()

    for far in range(1, nz):
        pl.when((z >= far - 1) & high)(lambda: signal(news.at[0], hist + nx, cand))
        pl.when((z + far - 1 < nz) & low)(lambda: signal(news.at[1], hist - nx, cand))
        pl.when(z >= far)(lambda: pl.semaphore_wait(news.at[0], 1))
        pl.when(z + far < nz)(lambda: pl.semaphore_wait(news.at[1], 1))

    def activate(block, p):
        weights = wuq[p * side // PIECES:(p + 1) * side // PIECES].reshape(span, width)
        return half_silu(times_rows(block, weights) * 0.5).astype(BF16)

    def z_copy(p, s):
        return remote(
            q_all.at[p, 0, 0], q_all.at[p, 0, s], z_ssem.at[p, s], z_rsem.at[p, s], (at(s, 0), cand)
        )

    def x_copy(p, t, s):
        return remote(
            q_all.at[p, 0, s], q_all.at[p, t, s], x_ssem.at[p, t, s], x_rsem.at[p, t, s],
            (at(0, t), cand),
        )

    def ret_copy(p):
        return remote(
            q_ret.at[p], q_all.at[p, 0, 0], ret_ssem.at[p], ret_rsem.at[p], (hist, partner)
        )

    def far_copy(p):
        return remote(
            q_ret.at[p], q_all.at[p, 0, half], far_ssem.at[p], z_rsem.at[p, half],
            (at(half, 0), partner),
        )

    def part_copy(p, t, s):
        return remote(
            part.at[p, t, s], landed.at[p, t, s], part_ssem.at[p, t, s], part_rsem.at[p, t, s],
            (at(s, t), cand),
        )

    u_copy = remote(u_send, u_own, u_sem.at[0], u_sem.at[1], (hist, partner))
    far_first = list(range(nz - 1, 0, -1))

    def pass_x(p, s):
        for t in range(1, nx):
            x_copy(p, t, s).start()

    load_wuq.wait()
    load_emb.wait()
    for step in range(1, side):
        wuq_copy(step).wait()
        w_copy(step).start()

    emb_copy.wait_recv()
    for p in range(PIECES):
        act = activate(embs[...].reshape(2 * rows, width), p)

        def queries():
            q_ret[p] = act[rows:]
            ret_copy(p).start()
            if p < DIRECT:
                far_copy(p).start()
            q_all[p, 0, 0] = act[:rows]
            for s in far_first:
                z_copy(p, s).start()
            pass_x(p, 0)

        def gates():
            cols = slice(p * span, (p + 1) * span)
            u_own[:, cols] = act[:rows]
            u_send[:, cols] = act[rows:]

        pl.when(is_q)(queries)
        pl.when(~is_q)(gates)
    wp_copy(1).start()

    for load in load_small:
        load.wait()
    users = jnp.broadcast_to(user_ref[...].astype(F32), (tile_rows, nh * rows)).T
    lane = lax.broadcasted_iota(jnp.int32, (nh * rows, tile_rows), 1)
    for tile in range(tiles):
        same = users == owner_ref[0, tile].astype(F32)
        valid = lane < len_ref[0, tile]
        block = jnp.where(same & valid, 1.0, 0.0).astype(BF16).reshape(nz, nx, rows, tile_rows)
        for zh in range(nz):
            for xh in range(nx):
                mask[flip(x, xh), flip(z, zh), :, tile * tile_rows:(tile + 1) * tile_rows] = block[
                    zh, xh
                ]

    scale = 0.5 / head_size**0.5
    load_kv.wait()

    def attend(p, t):
        allowed = mask[t].reshape(nz * rows, keys)
        for head in range(HEADS // PIECES):
            cols = slice(head * head_size, (head + 1) * head_size)
            here = slice(p * span + head * head_size, p * span + (head + 1) * head_size)
            q = q_all[p, t, :, :, cols].reshape(nz * rows, head_size)
            k = kv[:, 0, :, here].reshape(keys, head_size)
            v = kv[:, 1, :, here].reshape(keys, head_size)
            weights = half_silu(times_rows(q, k) * scale).astype(BF16) * allowed
            total = jnp.dot(weights, v, preferred_element_type=F32)
            part[p, t, :, :, cols] = total.astype(BF16).reshape(nz, rows, head_size)
        for s in far_first + [0]:
            if s or t:
                part_copy(p, t, s).start()

    def arrive(p, s):
        z_copy(p, s).wait_recv()
        pass_x(p, s)

    def spread_q():
        for p in range(PIECES):
            for s in range(1, nz):
                arrive(p, s)

    def spread_u():
        for p in range(PIECES):
            ret_copy(p).wait_recv()
            for s in far_first:
                if s != half or p >= DIRECT:
                    z_copy(p, s).start()
            pass_x(p, 0)
        u_copy.start()
        for p in range(PIECES):
            for s in range(1, nz):
                arrive(p, s)

    pl.when(is_q)(spread_q)
    pl.when(~is_q)(spread_u)
    for p in range(PIECES):
        attend(p, 0)
    for p in range(PIECES):
        for t in range(1, nx):
            for s in range(nz):
                x_copy(p, t, s).wait_recv()
            attend(p, t)

    for chunk in range(2):
        wp_copy(chunk).wait()
    for step in range(1, side):
        wf_copy(step).start()

    def sent_q():
        for p in range(PIECES):
            ret_copy(p).wait_send()
            if p < DIRECT:
                far_copy(p).wait_send()
                z_copy(p, half).wait_send()
        u_copy.wait_recv()

    pl.when(is_q)(sent_q)
    pl.when(~is_q)(lambda: u_copy.wait_send())
    emb_copy.wait_send()
    for p in range(PIECES):
        for s in range(1, nz):
            if s != half or p >= DIRECT:
                z_copy(p, s).wait_send()
        for t in range(1, nx):
            for s in range(nz):
                x_copy(p, t, s).wait_send()
    attn = []
    for p in range(PIECES):
        total = part[p, 0, 0].astype(F32)
        for t in range(nx):
            for s in range(nz):
                if s or t:
                    part_copy(p, t, s).wait()
                    total = total + landed[p, t, s].astype(F32)
        attn.append(total)
    attn = jnp.concatenate(attn, axis=1)
    center = jnp.mean(attn, axis=1, keepdims=True)
    variance = jnp.mean((attn - center) ** 2, axis=1, keepdims=True)
    normed = (attn - center) / jnp.sqrt(variance + 1e-05)
    y = (normed * u_own[...].astype(F32)).astype(BF16)

    load_wout.wait()
    for step in range(1, side):
        w_copy(step).wait()
        wf_copy(step).wait()
    projected = times_rows(y, wout[...].reshape(width, width))
    out_ref[0] = (embs[0].astype(F32) + projected).astype(BF16)


def solution(mesh):
    nh, nc = mesh.shape["hist"], mesh.shape["cand"]
    nx = 1 << ((nh.bit_length() - 1) // 2)
    nz = nh // nx

    def per_device(cand_emb, cand_user, kv_cache, tile_user, tile_len, w_uq, w_out):
        rows, width = cand_emb.shape[1:]
        tiles, _, tile_rows, _ = kv_cache.shape[1:]
        feats, outs = w_uq.shape[0], w_out.shape[0]
        side = nc // 2
        span = width // PIECES
        dma = pltpu.SemaphoreType.DMA
        hbm = pl.BlockSpec(memory_space=pl.ANY)
        vmem = pl.BlockSpec(memory_space=pltpu.VMEM)
        return pl.pallas_call(
            functools.partial(kernel, nx, nz, nc),
            out_shape=jax.ShapeDtypeStruct(cand_emb.shape, BF16),
            in_specs=[hbm] * 7,
            out_specs=vmem,
            scratch_shapes=[
                pltpu.VMEM(cand_user.shape, jnp.int32),
                pltpu.SMEM(tile_user.shape, jnp.int32),
                pltpu.SMEM(tile_len.shape, jnp.int32),
                pltpu.VMEM((2, rows, width), BF16),
                pltpu.VMEM((tiles, 2, tile_rows, width), BF16),
                pltpu.VMEM((side, feats, width), BF16),
                pltpu.VMEM((nc, outs, width), BF16),
                pltpu.VMEM((PIECES, rows, span), BF16),
                pltpu.VMEM((PIECES, nx, nz, rows, span), BF16),
                pltpu.VMEM((rows, width), BF16),
                pltpu.VMEM((rows, width), BF16),
                pltpu.VMEM((nx, nz, rows, tiles * tile_rows), BF16),
                pltpu.VMEM((PIECES, nx, nz, rows, span), BF16),
                pltpu.VMEM((PIECES, nx, nz, rows, span), BF16),
                dma((7,)),
                dma((2,)),
                dma((side,)), dma((side,)),
                dma((PIECES,)), dma((PIECES,)),
                dma((PIECES,)),
                dma((PIECES, nz)), dma((PIECES, nz)),
                dma((PIECES, nx, nz)), dma((PIECES, nx, nz)),
                dma((PIECES, nx, nz)), dma((PIECES, nx, nz)),
                dma((2,)),
                dma((side,)), dma((side,)),
                dma((2,)), dma((2,)),
                dma((side,)), dma((side,)),
                pltpu.SemaphoreType.REGULAR((2,)),
            ],
            compiler_params=pltpu.CompilerParams(collective_id=0, has_side_effects=True),
        )(cand_emb, cand_user, kv_cache, tile_user, tile_len, w_uq, w_out)

    in_specs = (
        P("cand", "hist", None),
        P("cand", None),
        P("cand", "hist", None, None, None),
        P("cand", "hist"),
        P("cand", "hist"),
        P("cand", None),
        P("cand", None),
    )
    return jax.shard_map(
        per_device, mesh=mesh, in_specs=in_specs, out_specs=P("cand", "hist", None), check_vma=False
    )
```

```python
import functools

import jax
import jax.numpy as jnp
from jax import lax
from jax.experimental import pallas as pl
from jax.experimental.pallas import tpu as pltpu
from jax.sharding import PartitionSpec as P

HEADS = 8
PIECES = 2
DIRECT = {(1, "far"), (0, "near")}
JOIN_X = (1,)
JOIN_Z = ()
BF16 = jnp.bfloat16
F32 = jnp.float32


def times_rows(left, slab):
    return lax.dot_general(left, slab, (((1,), (1,)), ((), ())), preferred_element_type=F32)


def half_silu(half):
    return half + half * jnp.tanh(half)


def flip(index, bits):
    bit = 1
    while bit <= bits:
        if bits & bit:
            index = index + bit * (1 - 2 * lax.rem(index // bit, 2))
        bit *= 2
    return index


def kernel(
    nx, nz, nc, emb_hbm, user_hbm, kv_hbm, owner_hbm, len_hbm, wuq_hbm, wout_hbm, out_ref,
    user_ref, owner_ref, len_ref, embs, kv, wuq, wout, q_ret, q_all, u_own, u_send, mask, part, landed, from_x, from_z,
    local_sem, emb_sem, wuq_ssem, wuq_rsem, ret_ssem, ret_rsem, far_ssem, z_ssem, z_rsem, x_ssem, x_rsem,
    part_ssem, part_rsem, jx_ssem, jx_rsem, jz_ssem, jz_rsem, u_sem, w_ssem, w_rsem, wp_ssem, wp_rsem, wf_ssem, wf_rsem, news,
):
    nh = nx * nz
    hist = lax.axis_index("hist")
    z, x = hist // nx, lax.rem(hist, nx)
    cand = lax.axis_index("cand")
    side = nc // 2
    is_q = cand >= side
    partner = lax.rem(cand + side, nc)
    place = lax.rem(cand, side)
    base = cand - place
    rows, width = embs.shape[1], embs.shape[2]
    head_size = width // HEADS
    tiles, tile_rows = kv.shape[0], kv.shape[2]
    keys = tiles * tile_rows
    span = width // PIECES
    half = nz // 2

    def remote(src, dst, ssem, rsem, peer):
        return pltpu.make_async_remote_copy(
            src_ref=src, dst_ref=dst, send_sem=ssem, recv_sem=rsem,
            device_id=peer, device_id_type=pl.DeviceIdType.MESH,
        )

    def at(s, t):
        return flip(z, s) * nx + flip(x, t)

    def mate(step):
        return base + lax.rem(place + step, side)

    def signal(sem, hist_to, cand_to):
        pl.semaphore_signal(
            sem, inc=1, device_id=(hist_to, cand_to), device_id_type=pl.DeviceIdType.MESH
        )

    load_emb = pltpu.make_async_copy(emb_hbm.at[0], embs.at[0], local_sem.at[0])
    load_wuq = pltpu.make_async_copy(wuq_hbm, wuq.at[place], local_sem.at[1])
    load_kv = pltpu.make_async_copy(kv_hbm.at[0], kv, local_sem.at[2])
    load_wout = pltpu.make_async_copy(wout_hbm, wout.at[cand], local_sem.at[3])
    load_small = [
        pltpu.make_async_copy(src, dst, local_sem.at[4 + index])
        for index, (src, dst) in enumerate(
            ((user_hbm, user_ref), (owner_hbm, owner_ref), (len_hbm, len_ref))
        )
    ]
    barrier = pltpu.get_barrier_semaphore()
    low, high = z > 0, z < nz - 1
    signal(barrier, hist, partner)
    for step in range(1, side):
        signal(barrier, hist, mate(step))
    for t in range(1, nx):
        signal(barrier, at(0, t), cand)
    pl.when(low)(lambda: signal(barrier, hist - nx, cand))
    pl.when(high)(lambda: signal(barrier, hist + nx, cand))
    load_emb.start()
    load_wuq.start()
    for load in load_small:
        load.start()
    load_wout.start()
    load_kv.start()
    pl.semaphore_wait(
        barrier, 1 + side - 1 + nx - 1 + low.astype(jnp.int32) + high.astype(jnp.int32)
    )

    emb_copy = remote(emb_hbm.at[0], embs.at[1], emb_sem.at[0], emb_sem.at[1], (hist, partner))
    emb_copy.start()

    def wuq_copy(step):
        return remote(
            wuq_hbm, wuq.at[place], wuq_ssem.at[step], wuq_rsem.at[step], (hist, mate(step))
        )

    for step in range(1, side):
        wuq_copy(step).start()

    outs = wout.shape[1]
    cuts = (0, outs // 4, outs)

    def w_copy(step):
        return remote(wout_hbm, wout.at[cand], w_ssem.at[step], w_rsem.at[step], (hist, mate(step)))

    def wp_copy(chunk):
        lines = pl.ds(cuts[chunk], cuts[chunk + 1] - cuts[chunk])
        return remote(
            wout_hbm.at[lines], wout.at[cand, lines], wp_ssem.at[chunk], wp_rsem.at[chunk],
            (hist, partner),
        )

    def wf_copy(step):
        return remote(
            wout.at[partner], wout.at[partner], wf_ssem.at[step], wf_rsem.at[step],
            (hist, mate(step)),
        )

    wp_copy(0).start()

    for far in range(1, nz):
        pl.when((z >= far - 1) & high)(lambda: signal(news.at[0], hist + nx, cand))
        pl.when((z + far - 1 < nz) & low)(lambda: signal(news.at[1], hist - nx, cand))
        pl.when(z >= far)(lambda: pl.semaphore_wait(news.at[0], 1))
        pl.when(z + far < nz)(lambda: pl.semaphore_wait(news.at[1], 1))

    def activate(block, p):
        weights = wuq[p * side // PIECES:(p + 1) * side // PIECES].reshape(span, width)
        return half_silu(times_rows(block, weights) * 0.5).astype(BF16)

    def z_copy(p, s):
        return remote(
            q_all.at[p, 0, 0], q_all.at[p, 0, s], z_ssem.at[p, s], z_rsem.at[p, s], (at(s, 0), cand)
        )

    def x_copy(p, t, s):
        return remote(
            q_all.at[p, 0, s], q_all.at[p, t, s], x_ssem.at[p, t, s], x_rsem.at[p, t, s],
            (at(0, t), cand),
        )

    def ret_copy(p):
        return remote(
            q_ret.at[p], q_all.at[p, 0, 0], ret_ssem.at[p], ret_rsem.at[p], (hist, partner)
        )

    def direct(p, s):
        return (p, {1: "near", half: "far", half + 1: "last"}.get(s)) in DIRECT

    def far_copy(p, s):
        return remote(
            q_ret.at[p], q_all.at[p, 0, s], far_ssem.at[p, s], z_rsem.at[p, s], (at(s, 0), partner)
        )

    def part_copy(p, t, s):
        return remote(
            part.at[p, t, s], landed.at[p, t, s], part_ssem.at[p, t, s], part_rsem.at[p, t, s],
            (at(s, t), cand),
        )

    def joins_x(p):
        return p in JOIN_X and nx > 1

    def joins_z(p):
        return p in JOIN_Z and nz > 2 and not joins_x(p)

    def path(p, t, s):
        if t == 0 and s >= half:
            if joins_x(p):
                return "x"
            if joins_z(p):
                return "z" if s % 2 else "later"
        return "part" if s or t else "own"

    def add(ref, more):
        ref[...] = (ref[...].astype(F32) + more.astype(F32)).astype(BF16)

    def jx_copy(p, s):
        return remote(
            part.at[p, 0, s], from_x.at[p, s - half], jx_ssem.at[p, s], jx_rsem.at[p, s],
            (at(0, 1), cand),
        )

    def jz_copy(p, s):
        return remote(
            part.at[p, 0, s], from_z.at[p, s - 1 - half], jz_ssem.at[p, s], jz_rsem.at[p, s],
            (at(1, 0), cand),
        )

    u_copy = remote(u_send, u_own, u_sem.at[0], u_sem.at[1], (hist, partner))
    far_first = list(range(nz - 1, 0, -1))

    def pass_x(p, s):
        for t in range(1, nx):
            x_copy(p, t, s).start()

    load_wuq.wait()
    load_emb.wait()
    for step in range(1, side):
        wuq_copy(step).wait()
        w_copy(step).start()

    emb_copy.wait_recv()
    for p in range(PIECES):
        act = activate(embs[...].reshape(2 * rows, width), p)

        def queries():
            q_ret[p] = act[rows:]
            ret_copy(p).start()
            for s in far_first:
                if direct(p, s):
                    far_copy(p, s).start()
            q_all[p, 0, 0] = act[:rows]
            for s in far_first:
                z_copy(p, s).start()
            pass_x(p, 0)

        def gates():
            cols = slice(p * span, (p + 1) * span)
            u_own[:, cols] = act[:rows]
            u_send[:, cols] = act[rows:]

        pl.when(is_q)(queries)
        pl.when(~is_q)(gates)
    wp_copy(1).start()

    for load in load_small:
        load.wait()
    users = jnp.broadcast_to(user_ref[...].astype(F32), (tile_rows, nh * rows)).T
    lane = lax.broadcasted_iota(jnp.int32, (nh * rows, tile_rows), 1)
    for tile in range(tiles):
        same = users == owner_ref[0, tile].astype(F32)
        valid = lane < len_ref[0, tile]
        block = jnp.where(same & valid, 1.0, 0.0).astype(BF16).reshape(nz, nx, rows, tile_rows)
        for zh in range(nz):
            for xh in range(nx):
                mask[flip(x, xh), flip(z, zh), :, tile * tile_rows:(tile + 1) * tile_rows] = block[
                    zh, xh
                ]

    scale = 0.5 / head_size**0.5
    load_kv.wait()

    def attend(p, t):
        allowed = mask[t].reshape(nz * rows, keys)
        for head in range(HEADS // PIECES):
            cols = slice(head * head_size, (head + 1) * head_size)
            here = slice(p * span + head * head_size, p * span + (head + 1) * head_size)
            q = q_all[p, t, :, :, cols].reshape(nz * rows, head_size)
            k = kv[:, 0, :, here].reshape(keys, head_size)
            v = kv[:, 1, :, here].reshape(keys, head_size)
            weights = half_silu(times_rows(q, k) * scale).astype(BF16) * allowed
            total = jnp.dot(weights, v, preferred_element_type=F32)
            part[p, t, :, :, cols] = total.astype(BF16).reshape(nz, rows, head_size)
        if t == 1 and joins_x(p):
            for s in range(half, nz):
                jx_copy(p, s).wait_recv()
            add(part.at[p, 1, pl.ds(half, nz - half)], from_x[p])
        for s in far_first + [0]:
            way = path(p, t, s)
            if way == "part":
                part_copy(p, t, s).start()
            elif way == "x":
                jx_copy(p, s).start()
            elif way == "z":
                jz_copy(p, s).start()

    def forward_z(p):
        for s in range(half, nz, 2):
            jz_copy(p, s + 1).wait_recv()
            add(part.at[p, 0, s], from_z[p, s - half])
            part_copy(p, 0, s).start()

    def arrive(p, s):
        z_copy(p, s).wait_recv()
        pass_x(p, s)

    def spread_q():
        for p in range(PIECES):
            for s in range(1, nz):
                arrive(p, s)

    def spread_u():
        for p in range(PIECES):
            ret_copy(p).wait_recv()
            for s in far_first:
                if not direct(p, s):
                    z_copy(p, s).start()
            pass_x(p, 0)
        u_copy.start()
        for p, s in ((p, s) for p in range(PIECES) for s in range(1, nz)):
            arrive(p, s)

    pl.when(is_q)(spread_q)
    pl.when(~is_q)(spread_u)
    for p in range(PIECES):
        attend(p, 0)
    for p in range(PIECES):
        for t in range(1, nx):
            for s in range(nz):
                x_copy(p, t, s).wait_recv()
            attend(p, t)
        if joins_z(p):
            forward_z(p)

    for chunk in range(2):
        wp_copy(chunk).wait()
    for step in range(1, side):
        wf_copy(step).start()

    def sent_q():
        for p in range(PIECES):
            ret_copy(p).wait_send()
            for s in range(1, nz):
                if direct(p, s):
                    far_copy(p, s).wait_send()
                    z_copy(p, s).wait_send()
        u_copy.wait_recv()

    pl.when(is_q)(sent_q)
    pl.when(~is_q)(lambda: u_copy.wait_send())
    emb_copy.wait_send()
    for p in range(PIECES):
        for s in range(1, nz):
            if not direct(p, s):
                z_copy(p, s).wait_send()
        for t in range(1, nx):
            for s in range(nz):
                x_copy(p, t, s).wait_send()
    totals = [part[p, 0, 0].astype(F32) for p in range(PIECES)]
    for t in range(nx):
        for p in range(PIECES):
            for s in range(nz):
                way = path(p, t, s)
                if way == "x":
                    jx_copy(p, s).wait_send()
                elif way == "z":
                    jz_copy(p, s).wait_send()
                elif way != "own":
                    part_copy(p, t, s).wait()
                    totals[p] = totals[p] + landed[p, t, s].astype(F32)
    attn = jnp.concatenate(totals, axis=1)
    center = jnp.mean(attn, axis=1, keepdims=True)
    variance = jnp.mean((attn - center) ** 2, axis=1, keepdims=True)
    normed = (attn - center) / jnp.sqrt(variance + 1e-05)
    y = (normed * u_own[...].astype(F32)).astype(BF16)

    load_wout.wait()
    for step in range(1, side):
        w_copy(step).wait()
        wf_copy(step).wait()
    projected = times_rows(y, wout[...].reshape(width, width))
    out_ref[0] = (embs[0].astype(F32) + projected).astype(BF16)


def solution(mesh):
    nh, nc = mesh.shape["hist"], mesh.shape["cand"]
    nx = 1 << ((nh.bit_length() - 1) // 2)
    nz = nh // nx

    def per_device(cand_emb, cand_user, kv_cache, tile_user, tile_len, w_uq, w_out):
        rows, width = cand_emb.shape[1:]
        tiles, _, tile_rows, _ = kv_cache.shape[1:]
        feats, outs = w_uq.shape[0], w_out.shape[0]
        side = nc // 2
        span = width // PIECES
        dma = pltpu.SemaphoreType.DMA
        hbm = pl.BlockSpec(memory_space=pl.ANY)
        vmem = pl.BlockSpec(memory_space=pltpu.VMEM)
        return pl.pallas_call(
            functools.partial(kernel, nx, nz, nc),
            out_shape=jax.ShapeDtypeStruct(cand_emb.shape, BF16),
            in_specs=[hbm] * 7,
            out_specs=vmem,
            scratch_shapes=[
                pltpu.VMEM(cand_user.shape, jnp.int32),
                pltpu.SMEM(tile_user.shape, jnp.int32),
                pltpu.SMEM(tile_len.shape, jnp.int32),
                pltpu.VMEM((2, rows, width), BF16),
                pltpu.VMEM((tiles, 2, tile_rows, width), BF16),
                pltpu.VMEM((side, feats, width), BF16),
                pltpu.VMEM((nc, outs, width), BF16),
                pltpu.VMEM((PIECES, rows, span), BF16),
                pltpu.VMEM((PIECES, nx, nz, rows, span), BF16),
                pltpu.VMEM((rows, width), BF16),
                pltpu.VMEM((rows, width), BF16),
                pltpu.VMEM((nx, nz, rows, tiles * tile_rows), BF16),
                pltpu.VMEM((PIECES, nx, nz, rows, span), BF16),
                pltpu.VMEM((PIECES, nx, nz, rows, span), BF16),
                pltpu.VMEM((PIECES, nz - nz // 2, rows, span), BF16),
                pltpu.VMEM((PIECES, nz - nz // 2, rows, span), BF16),
                dma((7,)),
                dma((2,)),
                dma((side,)), dma((side,)),
                dma((PIECES,)), dma((PIECES,)),
                dma((PIECES, nz)),
                dma((PIECES, nz)), dma((PIECES, nz)),
                dma((PIECES, nx, nz)), dma((PIECES, nx, nz)),
                dma((PIECES, nx, nz)), dma((PIECES, nx, nz)),
                dma((PIECES, nz)), dma((PIECES, nz)),
                dma((PIECES, nz)), dma((PIECES, nz)),
                dma((2,)),
                dma((side,)), dma((side,)),
                dma((2,)), dma((2,)),
                dma((side,)), dma((side,)),
                pltpu.SemaphoreType.REGULAR((2,)),
            ],
            compiler_params=pltpu.CompilerParams(collective_id=0, has_side_effects=True),
        )(cand_emb, cand_user, kv_cache, tile_user, tile_len, w_uq, w_out)

    in_specs = (
        P("cand", "hist", None),
        P("cand", None),
        P("cand", "hist", None, None, None),
        P("cand", "hist"),
        P("cand", "hist"),
        P("cand", None),
        P("cand", None),
    )
    return jax.shard_map(
        per_device, mesh=mesh, in_specs=in_specs, out_specs=P("cand", "hist", None), check_vma=False
    )
```

```python
import functools

import jax
import jax.numpy as jnp
from jax import lax
from jax.experimental import pallas as pl
from jax.experimental.pallas import tpu as pltpu
from jax.sharding import PartitionSpec as P

HEADS = 8
PIECES = 2
DIRECT = {(1, "far"), (0, "near")}
JOIN_X = (1,)
JOIN_Z = ()
BF16 = jnp.bfloat16
F32 = jnp.float32


def times_rows(left, slab):
    return lax.dot_general(left, slab, (((1,), (1,)), ((), ())), preferred_element_type=F32)


def half_silu(half):
    return half + half * jnp.tanh(half)


def flip(index, bits):
    bit = 1
    while bit <= bits:
        if bits & bit:
            index = index + bit * (1 - 2 * lax.rem(index // bit, 2))
        bit *= 2
    return index


def kernel(
    nx, nz, nc, emb_hbm, user_hbm, kv_hbm, owner_hbm, len_hbm, wuq_hbm, wout_hbm, out_ref,
    user_ref, owner_ref, len_ref, embs, kv, wuq, wout, q_ret, q_all, u_own, u_send, mask, part, landed, from_x, from_z,
    local_sem, emb_sem, wuq_ssem, wuq_rsem, ret_ssem, ret_rsem, far_ssem, z_ssem, z_rsem, x_ssem, x_rsem,
    part_ssem, part_rsem, jx_ssem, jx_rsem, jz_ssem, jz_rsem, u_sem, w_ssem, w_rsem, wp_ssem, wp_rsem, wf_ssem, wf_rsem, news,
):
    nh = nx * nz
    hist = lax.axis_index("hist")
    z, x = hist // nx, lax.rem(hist, nx)
    cand = lax.axis_index("cand")
    side = nc // 2
    is_q = cand >= side
    partner = lax.rem(cand + side, nc)
    place = lax.rem(cand, side)
    base = cand - place
    rows, width = embs.shape[1], embs.shape[2]
    head_size = width // HEADS
    tiles, tile_rows = kv.shape[0], kv.shape[2]
    keys = tiles * tile_rows
    span = width // PIECES
    half = nz // 2

    def remote(src, dst, ssem, rsem, peer):
        return pltpu.make_async_remote_copy(
            src_ref=src, dst_ref=dst, send_sem=ssem, recv_sem=rsem,
            device_id=peer, device_id_type=pl.DeviceIdType.MESH,
        )

    def at(s, t):
        return flip(z, s) * nx + flip(x, t)

    def mate(step):
        return base + lax.rem(place + step, side)

    def signal(sem, hist_to, cand_to):
        pl.semaphore_signal(
            sem, inc=1, device_id=(hist_to, cand_to), device_id_type=pl.DeviceIdType.MESH
        )

    load_emb = pltpu.make_async_copy(emb_hbm.at[0], embs.at[0], local_sem.at[0])
    load_wuq = pltpu.make_async_copy(wuq_hbm, wuq.at[place], local_sem.at[1])
    load_kv = pltpu.make_async_copy(kv_hbm.at[0], kv, local_sem.at[2])
    load_wout = pltpu.make_async_copy(wout_hbm, wout.at[cand], local_sem.at[3])
    load_small = [
        pltpu.make_async_copy(src, dst, local_sem.at[4 + index])
        for index, (src, dst) in enumerate(
            ((user_hbm, user_ref), (owner_hbm, owner_ref), (len_hbm, len_ref))
        )
    ]
    barrier = pltpu.get_barrier_semaphore()
    low, high = z > 0, z < nz - 1
    signal(barrier, hist, partner)
    for step in range(1, side):
        signal(barrier, hist, mate(step))
    for t in range(1, nx):
        signal(barrier, at(0, t), cand)
    pl.when(low)(lambda: signal(barrier, hist - nx, cand))
    pl.when(high)(lambda: signal(barrier, hist + nx, cand))
    load_emb.start()
    load_wuq.start()
    for load in load_small:
        load.start()
    load_wout.start()
    load_kv.start()
    pl.semaphore_wait(
        barrier, 1 + side - 1 + nx - 1 + low.astype(jnp.int32) + high.astype(jnp.int32)
    )

    emb_copy = remote(emb_hbm.at[0], embs.at[1], emb_sem.at[0], emb_sem.at[1], (hist, partner))
    emb_copy.start()

    def wuq_copy(step):
        return remote(
            wuq_hbm, wuq.at[place], wuq_ssem.at[step], wuq_rsem.at[step], (hist, mate(step))
        )

    for step in range(1, side):
        wuq_copy(step).start()

    outs = wout.shape[1]
    cuts = (0, outs // 4, outs)

    def w_copy(step):
        return remote(wout_hbm, wout.at[cand], w_ssem.at[step], w_rsem.at[step], (hist, mate(step)))

    def wp_copy(chunk):
        lines = pl.ds(cuts[chunk], cuts[chunk + 1] - cuts[chunk])
        return remote(
            wout_hbm.at[lines], wout.at[cand, lines], wp_ssem.at[chunk], wp_rsem.at[chunk],
            (hist, partner),
        )

    def wf_copy(step):
        return remote(
            wout.at[partner], wout.at[partner], wf_ssem.at[step], wf_rsem.at[step],
            (hist, mate(step)),
        )

    wp_copy(0).start()

    for far in range(1, nz):
        pl.when((z >= far - 1) & high)(lambda: signal(news.at[0], hist + nx, cand))
        pl.when((z + far - 1 < nz) & low)(lambda: signal(news.at[1], hist - nx, cand))
        pl.when(z >= far)(lambda: pl.semaphore_wait(news.at[0], 1))
        pl.when(z + far < nz)(lambda: pl.semaphore_wait(news.at[1], 1))

    def activate(block, p):
        weights = wuq[p * side // PIECES:(p + 1) * side // PIECES].reshape(span, width)
        return half_silu(times_rows(block, weights) * 0.5).astype(BF16)

    def z_copy(p, s):
        return remote(
            q_all.at[p, 0, 0], q_all.at[p, 0, s], z_ssem.at[p, s], z_rsem.at[p, s], (at(s, 0), cand)
        )

    def x_copy(p, t, s):
        return remote(
            q_all.at[p, 0, s], q_all.at[p, t, s], x_ssem.at[p, t, s], x_rsem.at[p, t, s],
            (at(0, t), cand),
        )

    def ret_copy(p):
        return remote(
            q_ret.at[p], q_all.at[p, 0, 0], ret_ssem.at[p], ret_rsem.at[p], (hist, partner)
        )

    def direct(p, s):
        return (p, {1: "near", half: "far", half + 1: "last"}.get(s)) in DIRECT

    def far_copy(p, s):
        return remote(
            q_ret.at[p], q_all.at[p, 0, s], far_ssem.at[p, s], z_rsem.at[p, s], (at(s, 0), partner)
        )

    def part_copy(p, t, s):
        return remote(
            part.at[p, t, s], landed.at[p, t, s], part_ssem.at[p, t, s], part_rsem.at[p, t, s],
            (at(s, t), cand),
        )

    def joins_x(p):
        return p in JOIN_X and nx > 1

    def joins_z(p):
        return p in JOIN_Z and nz > 2 and not joins_x(p)

    def path(p, t, s):
        if t == 0 and s >= half:
            if joins_x(p):
                return "x"
            if joins_z(p):
                return "z" if s % 2 else "later"
        return "part" if s or t else "own"

    def add(ref, more):
        ref[...] = (ref[...].astype(F32) + more.astype(F32)).astype(BF16)

    def jx_copy(p, s):
        return remote(
            part.at[p, 0, s], from_x.at[p, s - half], jx_ssem.at[p, s], jx_rsem.at[p, s],
            (at(0, 1), cand),
        )

    def jz_copy(p, s):
        return remote(
            part.at[p, 0, s], from_z.at[p, s - 1 - half], jz_ssem.at[p, s], jz_rsem.at[p, s],
            (at(1, 0), cand),
        )

    u_copy = remote(u_send, u_own, u_sem.at[0], u_sem.at[1], (hist, partner))
    far_first = list(range(nz - 1, 0, -1))

    def pass_x(p, s):
        for t in range(1, nx):
            x_copy(p, t, s).start()

    load_wuq.wait()
    load_emb.wait()
    for step in range(1, side):
        wuq_copy(step).wait()
        w_copy(step).start()

    emb_copy.wait_recv()
    for p in range(PIECES):
        act = activate(embs[...].reshape(2 * rows, width), p)

        def queries():
            q_ret[p] = act[rows:]
            ret_copy(p).start()
            for s in far_first:
                if direct(p, s):
                    far_copy(p, s).start()
            q_all[p, 0, 0] = act[:rows]
            for s in far_first:
                z_copy(p, s).start()
            pass_x(p, 0)

        def gates():
            cols = slice(p * span, (p + 1) * span)
            u_own[:, cols] = act[:rows]
            u_send[:, cols] = act[rows:]

        pl.when(is_q)(queries)
        pl.when(~is_q)(gates)
    wp_copy(1).start()

    for load in load_small:
        load.wait()
    users = jnp.broadcast_to(user_ref[...].astype(F32), (tile_rows, nh * rows)).T
    lane = lax.broadcasted_iota(jnp.int32, (nh * rows, tile_rows), 1)
    for tile in range(tiles):
        same = users == owner_ref[0, tile].astype(F32)
        valid = lane < len_ref[0, tile]
        block = jnp.where(same & valid, 1.0, 0.0).astype(BF16).reshape(nz, nx, rows, tile_rows)
        for zh in range(nz):
            for xh in range(nx):
                mask[flip(x, xh), flip(z, zh), :, tile * tile_rows:(tile + 1) * tile_rows] = block[
                    zh, xh
                ]

    scale = 0.5 / head_size**0.5
    load_kv.wait()

    def attend(p, t):
        allowed = mask[t].reshape(nz * rows, keys)
        for head in range(HEADS // PIECES):
            cols = slice(head * head_size, (head + 1) * head_size)
            here = slice(p * span + head * head_size, p * span + (head + 1) * head_size)
            q = q_all[p, t, :, :, cols].reshape(nz * rows, head_size)
            k = kv[:, 0, :, here].reshape(keys, head_size)
            v = kv[:, 1, :, here].reshape(keys, head_size)
            weights = half_silu(times_rows(q, k) * scale).astype(BF16) * allowed
            total = jnp.dot(weights, v, preferred_element_type=F32)
            part[p, t, :, :, cols] = total.astype(BF16).reshape(nz, rows, head_size)
        if t == 1 and joins_x(p):
            for s in range(half, nz):
                jx_copy(p, s).wait_recv()
            add(part.at[p, 1, pl.ds(half, nz - half)], from_x[p])
        for s in list(range(half, nz)) + list(range(half)):
            way = path(p, t, s)
            if way == "part":
                part_copy(p, t, s).start()
            elif way == "x":
                jx_copy(p, s).start()
            elif way == "z":
                jz_copy(p, s).start()

    def forward_z(p):
        for s in range(half, nz, 2):
            jz_copy(p, s + 1).wait_recv()
            add(part.at[p, 0, s], from_z[p, s - half])
            part_copy(p, 0, s).start()

    def arrive(p, s):
        z_copy(p, s).wait_recv()
        pass_x(p, s)

    def spread_q():
        for p in range(PIECES):
            for s in range(1, nz):
                arrive(p, s)

    def spread_u():
        for p in range(PIECES):
            ret_copy(p).wait_recv()
            for s in far_first:
                if not direct(p, s):
                    z_copy(p, s).start()
            pass_x(p, 0)
        u_copy.start()
        for p, s in ((p, s) for p in range(PIECES) for s in range(1, nz)):
            arrive(p, s)

    pl.when(is_q)(spread_q)
    pl.when(~is_q)(spread_u)
    for p in reversed(range(PIECES)):
        attend(p, 0)
    for p in range(PIECES):
        for t in range(1, nx):
            for s in range(nz):
                x_copy(p, t, s).wait_recv()
            attend(p, t)
        if joins_z(p):
            forward_z(p)

    for chunk in range(2):
        wp_copy(chunk).wait()
    for step in range(1, side):
        wf_copy(step).start()

    def sent_q():
        for p in range(PIECES):
            ret_copy(p).wait_send()
            for s in range(1, nz):
                if direct(p, s):
                    far_copy(p, s).wait_send()
                    z_copy(p, s).wait_send()
        u_copy.wait_recv()

    pl.when(is_q)(sent_q)
    pl.when(~is_q)(lambda: u_copy.wait_send())
    emb_copy.wait_send()
    for p in range(PIECES):
        for s in range(1, nz):
            if not direct(p, s):
                z_copy(p, s).wait_send()
        for t in range(1, nx):
            for s in range(nz):
                x_copy(p, t, s).wait_send()
    totals = [part[p, 0, 0].astype(F32) for p in range(PIECES)]
    for t in range(nx):
        for p in range(PIECES):
            for s in range(nz):
                way = path(p, t, s)
                if way == "x":
                    jx_copy(p, s).wait_send()
                elif way == "z":
                    jz_copy(p, s).wait_send()
                elif way != "own":
                    part_copy(p, t, s).wait()
                    totals[p] = totals[p] + landed[p, t, s].astype(F32)
    attn = jnp.concatenate(totals, axis=1)
    center = jnp.mean(attn, axis=1, keepdims=True)
    variance = jnp.mean((attn - center) ** 2, axis=1, keepdims=True)
    normed = (attn - center) / jnp.sqrt(variance + 1e-05)
    y = (normed * u_own[...].astype(F32)).astype(BF16)

    load_wout.wait()
    for step in range(1, side):
        w_copy(step).wait()
        wf_copy(step).wait()
    projected = times_rows(y, wout[...].reshape(width, width))
    out_ref[0] = (embs[0].astype(F32) + projected).astype(BF16)


def solution(mesh):
    nh, nc = mesh.shape["hist"], mesh.shape["cand"]
    nx = 1 << ((nh.bit_length() - 1) // 2)
    nz = nh // nx

    def per_device(cand_emb, cand_user, kv_cache, tile_user, tile_len, w_uq, w_out):
        rows, width = cand_emb.shape[1:]
        tiles, _, tile_rows, _ = kv_cache.shape[1:]
        feats, outs = w_uq.shape[0], w_out.shape[0]
        side = nc // 2
        span = width // PIECES
        dma = pltpu.SemaphoreType.DMA
        hbm = pl.BlockSpec(memory_space=pl.ANY)
        vmem = pl.BlockSpec(memory_space=pltpu.VMEM)
        return pl.pallas_call(
            functools.partial(kernel, nx, nz, nc),
            out_shape=jax.ShapeDtypeStruct(cand_emb.shape, BF16),
            in_specs=[hbm] * 7,
            out_specs=vmem,
            scratch_shapes=[
                pltpu.VMEM(cand_user.shape, jnp.int32),
                pltpu.SMEM(tile_user.shape, jnp.int32),
                pltpu.SMEM(tile_len.shape, jnp.int32),
                pltpu.VMEM((2, rows, width), BF16),
                pltpu.VMEM((tiles, 2, tile_rows, width), BF16),
                pltpu.VMEM((side, feats, width), BF16),
                pltpu.VMEM((nc, outs, width), BF16),
                pltpu.VMEM((PIECES, rows, span), BF16),
                pltpu.VMEM((PIECES, nx, nz, rows, span), BF16),
                pltpu.VMEM((rows, width), BF16),
                pltpu.VMEM((rows, width), BF16),
                pltpu.VMEM((nx, nz, rows, tiles * tile_rows), BF16),
                pltpu.VMEM((PIECES, nx, nz, rows, span), BF16),
                pltpu.VMEM((PIECES, nx, nz, rows, span), BF16),
                pltpu.VMEM((PIECES, nz - nz // 2, rows, span), BF16),
                pltpu.VMEM((PIECES, nz - nz // 2, rows, span), BF16),
                dma((7,)),
                dma((2,)),
                dma((side,)), dma((side,)),
                dma((PIECES,)), dma((PIECES,)),
                dma((PIECES, nz)),
                dma((PIECES, nz)), dma((PIECES, nz)),
                dma((PIECES, nx, nz)), dma((PIECES, nx, nz)),
                dma((PIECES, nx, nz)), dma((PIECES, nx, nz)),
                dma((PIECES, nz)), dma((PIECES, nz)),
                dma((PIECES, nz)), dma((PIECES, nz)),
                dma((2,)),
                dma((side,)), dma((side,)),
                dma((2,)), dma((2,)),
                dma((side,)), dma((side,)),
                pltpu.SemaphoreType.REGULAR((2,)),
            ],
            compiler_params=pltpu.CompilerParams(collective_id=0, has_side_effects=True),
        )(cand_emb, cand_user, kv_cache, tile_user, tile_len, w_uq, w_out)

    in_specs = (
        P("cand", "hist", None),
        P("cand", None),
        P("cand", "hist", None, None, None),
        P("cand", "hist"),
        P("cand", "hist"),
        P("cand", None),
        P("cand", None),
    )
    return jax.shard_map(
        per_device, mesh=mesh, in_specs=in_specs, out_specs=P("cand", "hist", None), check_vma=False
    )
```

```python
import functools

import jax
import jax.numpy as jnp
from jax import lax
from jax.experimental import pallas as pl
from jax.experimental.pallas import tpu as pltpu
from jax.sharding import PartitionSpec as P

HEADS = 8
PIECES = 2
DIRECT = {(1, "far"), (0, "near")}
JOIN_X = (1,)
JOIN_Z = ()
BF16 = jnp.bfloat16
F32 = jnp.float32


def times_rows(left, slab):
    return lax.dot_general(left, slab, (((1,), (1,)), ((), ())), preferred_element_type=F32)


def half_silu(half):
    return half + half * jnp.tanh(half)


def flip(index, bits):
    bit = 1
    while bit <= bits:
        if bits & bit:
            index = index + bit * (1 - 2 * lax.rem(index // bit, 2))
        bit *= 2
    return index


def kernel(
    nx, nz, nc, emb_hbm, user_hbm, kv_hbm, owner_hbm, len_hbm, wuq_hbm, wout_hbm, out_ref,
    user_ref, owner_ref, len_ref, embs, kv, wuq, wout, q_ret, q_all, u_own, u_send, mask, part, landed, from_x, from_z,
    local_sem, emb_sem, wuq_ssem, wuq_rsem, ret_ssem, ret_rsem, far_ssem, z_ssem, z_rsem, x_ssem, x_rsem,
    part_ssem, part_rsem, jx_ssem, jx_rsem, jz_ssem, jz_rsem, u_sem, w_ssem, w_rsem, wp_ssem, wp_rsem, wf_ssem, wf_rsem, news,
):
    nh = nx * nz
    hist = lax.axis_index("hist")
    z, x = hist // nx, lax.rem(hist, nx)
    cand = lax.axis_index("cand")
    side = nc // 2
    is_q = cand >= side
    partner = lax.rem(cand + side, nc)
    place = lax.rem(cand, side)
    base = cand - place
    rows, width = embs.shape[1], embs.shape[2]
    head_size = width // HEADS
    tiles, tile_rows = kv.shape[0], kv.shape[2]
    keys = tiles * tile_rows
    span = width // PIECES
    half = nz // 2

    def remote(src, dst, ssem, rsem, peer):
        return pltpu.make_async_remote_copy(
            src_ref=src, dst_ref=dst, send_sem=ssem, recv_sem=rsem,
            device_id=peer, device_id_type=pl.DeviceIdType.MESH,
        )

    def at(s, t):
        return flip(z, s) * nx + flip(x, t)

    def mate(step):
        return base + lax.rem(place + step, side)

    def signal(sem, hist_to, cand_to):
        pl.semaphore_signal(
            sem, inc=1, device_id=(hist_to, cand_to), device_id_type=pl.DeviceIdType.MESH
        )

    load_emb = pltpu.make_async_copy(emb_hbm.at[0], embs.at[0], local_sem.at[0])
    load_wuq = pltpu.make_async_copy(wuq_hbm, wuq.at[place], local_sem.at[1])
    load_kv = pltpu.make_async_copy(kv_hbm.at[0], kv, local_sem.at[2])
    load_wout = pltpu.make_async_copy(wout_hbm, wout.at[cand], local_sem.at[3])
    load_small = [
        pltpu.make_async_copy(src, dst, local_sem.at[4 + index])
        for index, (src, dst) in enumerate(
            ((user_hbm, user_ref), (owner_hbm, owner_ref), (len_hbm, len_ref))
        )
    ]
    barrier = pltpu.get_barrier_semaphore()
    low, high = z > 0, z < nz - 1
    signal(barrier, hist, partner)
    for step in range(1, side):
        signal(barrier, hist, mate(step))
    for t in range(1, nx):
        signal(barrier, at(0, t), cand)
    pl.when(low)(lambda: signal(barrier, hist - nx, cand))
    pl.when(high)(lambda: signal(barrier, hist + nx, cand))
    load_emb.start()
    load_wuq.start()
    for load in load_small:
        load.start()
    load_wout.start()
    load_kv.start()
    pl.semaphore_wait(
        barrier, 1 + side - 1 + nx - 1 + low.astype(jnp.int32) + high.astype(jnp.int32)
    )

    emb_copy = remote(emb_hbm.at[0], embs.at[1], emb_sem.at[0], emb_sem.at[1], (hist, partner))
    emb_copy.start()

    def wuq_copy(step):
        return remote(
            wuq_hbm, wuq.at[place], wuq_ssem.at[step], wuq_rsem.at[step], (hist, mate(step))
        )

    for step in range(1, side):
        wuq_copy(step).start()

    outs = wout.shape[1]
    cuts = (0, outs // 4, outs)

    def w_copy(step):
        return remote(wout_hbm, wout.at[cand], w_ssem.at[step], w_rsem.at[step], (hist, mate(step)))

    def wp_copy(chunk):
        lines = pl.ds(cuts[chunk], cuts[chunk + 1] - cuts[chunk])
        return remote(
            wout_hbm.at[lines], wout.at[cand, lines], wp_ssem.at[chunk], wp_rsem.at[chunk],
            (hist, partner),
        )

    def wf_copy(step):
        return remote(
            wout.at[partner], wout.at[partner], wf_ssem.at[step], wf_rsem.at[step],
            (hist, mate(step)),
        )

    wp_copy(0).start()
    pl.when(~is_q)(lambda: wp_copy(1).start())

    for far in range(1, nz):
        pl.when((z >= far - 1) & high)(lambda: signal(news.at[0], hist + nx, cand))
        pl.when((z + far - 1 < nz) & low)(lambda: signal(news.at[1], hist - nx, cand))
        pl.when(z >= far)(lambda: pl.semaphore_wait(news.at[0], 1))
        pl.when(z + far < nz)(lambda: pl.semaphore_wait(news.at[1], 1))

    def activate(block, p):
        weights = wuq[p * side // PIECES:(p + 1) * side // PIECES].reshape(span, width)
        return half_silu(times_rows(block, weights) * 0.5).astype(BF16)

    def z_copy(p, s):
        return remote(
            q_all.at[p, 0, 0], q_all.at[p, 0, s], z_ssem.at[p, s], z_rsem.at[p, s], (at(s, 0), cand)
        )

    def x_copy(p, t, s):
        return remote(
            q_all.at[p, 0, s], q_all.at[p, t, s], x_ssem.at[p, t, s], x_rsem.at[p, t, s],
            (at(0, t), cand),
        )

    def ret_copy(p):
        return remote(
            q_ret.at[p], q_all.at[p, 0, 0], ret_ssem.at[p], ret_rsem.at[p], (hist, partner)
        )

    def direct(p, s):
        return (p, {1: "near", half: "far", half + 1: "last"}.get(s)) in DIRECT

    def far_copy(p, s):
        return remote(
            q_ret.at[p], q_all.at[p, 0, s], far_ssem.at[p, s], z_rsem.at[p, s], (at(s, 0), partner)
        )

    def part_copy(p, t, s):
        return remote(
            part.at[p, t, s], landed.at[p, t, s], part_ssem.at[p, t, s], part_rsem.at[p, t, s],
            (at(s, t), cand),
        )

    def joins_x(p):
        return p in JOIN_X and nx > 1

    def joins_z(p):
        return p in JOIN_Z and nz > 2 and not joins_x(p)

    def path(p, t, s):
        if t == 0 and s >= half:
            if joins_x(p):
                return "x"
            if joins_z(p):
                return "z" if s % 2 else "later"
        return "part" if s or t else "own"

    def add(ref, more):
        ref[...] = (ref[...].astype(F32) + more.astype(F32)).astype(BF16)

    def jx_copy(p, s):
        return remote(
            part.at[p, 0, s], from_x.at[p, s - half], jx_ssem.at[p, s], jx_rsem.at[p, s],
            (at(0, 1), cand),
        )

    def jz_copy(p, s):
        return remote(
            part.at[p, 0, s], from_z.at[p, s - 1 - half], jz_ssem.at[p, s], jz_rsem.at[p, s],
            (at(1, 0), cand),
        )

    u_copy = remote(u_send, u_own, u_sem.at[0], u_sem.at[1], (hist, partner))
    far_first = list(range(nz - 1, 0, -1))

    def pass_x(p, s):
        for t in range(1, nx):
            x_copy(p, t, s).start()

    load_wuq.wait()
    load_emb.wait()
    for step in range(1, side):
        wuq_copy(step).wait()
        w_copy(step).start()

    emb_copy.wait_recv()
    for p in range(PIECES):
        act = activate(embs[...].reshape(2 * rows, width), p)

        def queries():
            q_ret[p] = act[rows:]
            ret_copy(p).start()
            for s in far_first:
                if direct(p, s):
                    far_copy(p, s).start()
            q_all[p, 0, 0] = act[:rows]
            for s in far_first:
                z_copy(p, s).start()
            pass_x(p, 0)

        def gates():
            cols = slice(p * span, (p + 1) * span)
            u_own[:, cols] = act[:rows]
            u_send[:, cols] = act[rows:]

        pl.when(is_q)(queries)
        pl.when(~is_q)(gates)
    pl.when(is_q)(lambda: wp_copy(1).start())

    for load in load_small:
        load.wait()
    users = jnp.broadcast_to(user_ref[...].astype(F32), (tile_rows, nh * rows)).T
    lane = lax.broadcasted_iota(jnp.int32, (nh * rows, tile_rows), 1)
    for tile in range(tiles):
        same = users == owner_ref[0, tile].astype(F32)
        valid = lane < len_ref[0, tile]
        block = jnp.where(same & valid, 1.0, 0.0).astype(BF16).reshape(nz, nx, rows, tile_rows)
        for zh in range(nz):
            for xh in range(nx):
                mask[flip(x, xh), flip(z, zh), :, tile * tile_rows:(tile + 1) * tile_rows] = block[
                    zh, xh
                ]

    scale = 0.5 / head_size**0.5
    load_kv.wait()

    def attend(p, t):
        allowed = mask[t].reshape(nz * rows, keys)
        for head in range(HEADS // PIECES):
            cols = slice(head * head_size, (head + 1) * head_size)
            here = slice(p * span + head * head_size, p * span + (head + 1) * head_size)
            q = q_all[p, t, :, :, cols].reshape(nz * rows, head_size)
            k = kv[:, 0, :, here].reshape(keys, head_size)
            v = kv[:, 1, :, here].reshape(keys, head_size)
            weights = half_silu(times_rows(q, k) * scale).astype(BF16) * allowed
            total = jnp.dot(weights, v, preferred_element_type=F32)
            part[p, t, :, :, cols] = total.astype(BF16).reshape(nz, rows, head_size)
        if t == 1 and joins_x(p):
            for s in range(half, nz):
                jx_copy(p, s).wait_recv()
            add(part.at[p, 1, pl.ds(half, nz - half)], from_x[p])
        for s in list(range(half, nz)) + list(range(half)):
            way = path(p, t, s)
            if way == "part":
                part_copy(p, t, s).start()
            elif way == "x":
                jx_copy(p, s).start()
            elif way == "z":
                jz_copy(p, s).start()

    def forward_z(p):
        for s in range(half, nz, 2):
            jz_copy(p, s + 1).wait_recv()
            add(part.at[p, 0, s], from_z[p, s - half])
            part_copy(p, 0, s).start()

    def arrive(p, s):
        z_copy(p, s).wait_recv()
        pass_x(p, s)

    def spread_q():
        for p in range(PIECES):
            for s in range(1, nz):
                arrive(p, s)

    def spread_u():
        for p in range(PIECES):
            ret_copy(p).wait_recv()
            for s in far_first:
                if not direct(p, s):
                    z_copy(p, s).start()
            pass_x(p, 0)
        u_copy.start()
        for p, s in ((p, s) for p in range(PIECES) for s in range(1, nz)):
            arrive(p, s)

    pl.when(is_q)(spread_q)
    pl.when(~is_q)(spread_u)
    for p in reversed(range(PIECES)):
        attend(p, 0)
    for p in range(PIECES):
        for t in range(1, nx):
            for s in range(nz):
                x_copy(p, t, s).wait_recv()
            attend(p, t)
        if joins_z(p):
            forward_z(p)

    for chunk in range(2):
        wp_copy(chunk).wait()
    for step in range(1, side):
        wf_copy(step).start()

    def sent_q():
        for p in range(PIECES):
            ret_copy(p).wait_send()
            for s in range(1, nz):
                if direct(p, s):
                    far_copy(p, s).wait_send()
                    z_copy(p, s).wait_send()
        u_copy.wait_recv()

    pl.when(is_q)(sent_q)
    pl.when(~is_q)(lambda: u_copy.wait_send())
    emb_copy.wait_send()
    for p in range(PIECES):
        for s in range(1, nz):
            if not direct(p, s):
                z_copy(p, s).wait_send()
        for t in range(1, nx):
            for s in range(nz):
                x_copy(p, t, s).wait_send()
    totals = [part[p, 0, 0].astype(F32) for p in range(PIECES)]
    for t in range(nx):
        for p in range(PIECES):
            for s in range(nz):
                way = path(p, t, s)
                if way == "x":
                    jx_copy(p, s).wait_send()
                elif way == "z":
                    jz_copy(p, s).wait_send()
                elif way != "own":
                    part_copy(p, t, s).wait()
                    totals[p] = totals[p] + landed[p, t, s].astype(F32)
    attn = jnp.concatenate(totals, axis=1)
    center = jnp.mean(attn, axis=1, keepdims=True)
    variance = jnp.mean((attn - center) ** 2, axis=1, keepdims=True)
    normed = (attn - center) / jnp.sqrt(variance + 1e-05)
    y = (normed * u_own[...].astype(F32)).astype(BF16)

    load_wout.wait()
    for step in range(1, side):
        w_copy(step).wait()
        wf_copy(step).wait()
    projected = times_rows(y, wout[...].reshape(width, width))
    out_ref[0] = (embs[0].astype(F32) + projected).astype(BF16)


def solution(mesh):
    nh, nc = mesh.shape["hist"], mesh.shape["cand"]
    nx = 1 << ((nh.bit_length() - 1) // 2)
    nz = nh // nx

    def per_device(cand_emb, cand_user, kv_cache, tile_user, tile_len, w_uq, w_out):
        rows, width = cand_emb.shape[1:]
        tiles, _, tile_rows, _ = kv_cache.shape[1:]
        feats, outs = w_uq.shape[0], w_out.shape[0]
        side = nc // 2
        span = width // PIECES
        dma = pltpu.SemaphoreType.DMA
        hbm = pl.BlockSpec(memory_space=pl.ANY)
        vmem = pl.BlockSpec(memory_space=pltpu.VMEM)
        return pl.pallas_call(
            functools.partial(kernel, nx, nz, nc),
            out_shape=jax.ShapeDtypeStruct(cand_emb.shape, BF16),
            in_specs=[hbm] * 7,
            out_specs=vmem,
            scratch_shapes=[
                pltpu.VMEM(cand_user.shape, jnp.int32),
                pltpu.SMEM(tile_user.shape, jnp.int32),
                pltpu.SMEM(tile_len.shape, jnp.int32),
                pltpu.VMEM((2, rows, width), BF16),
                pltpu.VMEM((tiles, 2, tile_rows, width), BF16),
                pltpu.VMEM((side, feats, width), BF16),
                pltpu.VMEM((nc, outs, width), BF16),
                pltpu.VMEM((PIECES, rows, span), BF16),
                pltpu.VMEM((PIECES, nx, nz, rows, span), BF16),
                pltpu.VMEM((rows, width), BF16),
                pltpu.VMEM((rows, width), BF16),
                pltpu.VMEM((nx, nz, rows, tiles * tile_rows), BF16),
                pltpu.VMEM((PIECES, nx, nz, rows, span), BF16),
                pltpu.VMEM((PIECES, nx, nz, rows, span), BF16),
                pltpu.VMEM((PIECES, nz - nz // 2, rows, span), BF16),
                pltpu.VMEM((PIECES, nz - nz // 2, rows, span), BF16),
                dma((7,)),
                dma((2,)),
                dma((side,)), dma((side,)),
                dma((PIECES,)), dma((PIECES,)),
                dma((PIECES, nz)),
                dma((PIECES, nz)), dma((PIECES, nz)),
                dma((PIECES, nx, nz)), dma((PIECES, nx, nz)),
                dma((PIECES, nx, nz)), dma((PIECES, nx, nz)),
                dma((PIECES, nz)), dma((PIECES, nz)),
                dma((PIECES, nz)), dma((PIECES, nz)),
                dma((2,)),
                dma((side,)), dma((side,)),
                dma((2,)), dma((2,)),
                dma((side,)), dma((side,)),
                pltpu.SemaphoreType.REGULAR((2,)),
            ],
            compiler_params=pltpu.CompilerParams(collective_id=0, has_side_effects=True),
        )(cand_emb, cand_user, kv_cache, tile_user, tile_len, w_uq, w_out)

    in_specs = (
        P("cand", "hist", None),
        P("cand", None),
        P("cand", "hist", None, None, None),
        P("cand", "hist"),
        P("cand", "hist"),
        P("cand", None),
        P("cand", None),
    )
    return jax.shard_map(
        per_device, mesh=mesh, in_specs=in_specs, out_specs=P("cand", "hist", None), check_vma=False
    )
```
